32 devices in a mesh: dp: 2 (over y), ctx: 4 (over x, core), tensor: 4 (over z).
Axes of the slice: x: 2, y: 2, z: 4, core: 2. Of those that a mesh axis runs over, the one named last changes fastest.
Arguments:
- residual: bfloat16 [2048, 3584], P(('dp', 'ctx', 'tensor')), parts along dimension 0, may hold values from -6 to 6
- queries: bfloat16 [2048, 1024], P(('dp', 'ctx'), 'tensor'), parts along dimension 0, may hold values from -8 to 8
- key_heads: bfloat16 [2048, 512], P(('dp', 'ctx'), 'tensor'), parts along dimension 0, may hold values from -8 to 8
- value_heads: bfloat16 [2048, 512], P(('dp', 'ctx'), 'tensor'), parts along dimension 0, may hold values from -6 to 6
- doc_blocks: int32 [12], P('dp'), parts along dimension 0, may hold values from 1 to 16, 32 in all
- out_weight: bfloat16 [1024, 3584], P('tensor'), may hold values from -0.53125 to 0.53125
- post_gain: float32 [3584], replicated, may hold values from 0.1 to 1.9
- ffn_gain: float32 [3584], replicated, may hold values from 0.1 to 1.9
- gate_weight: bfloat16 [3584, 3584], P('ctx', 'tensor'), may hold values from -0.09375 to 0.09375
- up_weight: bfloat16 [3584, 3584], P('ctx', 'tensor'), may hold values from -0.09375 to 0.09375
Outputs:
- mixed_stream: bfloat16 [2048, 3584], P(('dp', 'ctx', 'tensor')), parts along dimension 0
- ffn_hidden: bfloat16 [2048, 3584], P(('dp', 'ctx'), 'tensor'), parts along dimension 0
The draws below stay inside these ranges and needn't reach their ends.
There are 2 independent parts, one for each index of `dp`. The reference program is written for one: setup_inputs(seed, part) draws one part's arguments, and reference() takes and returns one part's arrays. A program takes and returns all parts, laid end to end along the dimension named above; an argument that names none is the same for every part. Nothing has to cross between parts.
Inputs may be any that keep to these rules, and one draw needn't show every extreme that they name: `doc_blocks`: the lengths, in blocks of 32 positions, of the 6 documents packed in order into the sequence; they sum to 32, and the longest has exactly 16 blocks.
All inputs are finite; a program needn't handle non-finite values.
Results may differ from the reference program's by a relative error of at most 0.025.
Values may be sent and summed in bfloat16 or wider, within the bound.
A program may use at most 64 MiB of HBM per device.

```python
import math
import jax
import jax.numpy as jnp
import numpy as np
from jax import lax

D = 3584
HD = 256
H = 4
KVH = 2
FF = 3584
TOK_CTX = 256
LENGTH = 1024
BLOCK = 32
NBLK = 32
DOCS = 6
MOST_BLK = 16


def draw_out_weight(key, part):
    fan_rows = H * HD
    drawn = jnp.clip(jax.random.normal(key, (fan_rows, D), jnp.float32), -5.0, 5.0) * fan_rows ** (-0.5)
    return drawn.astype(jnp.bfloat16)


def background(key, array_shape):
    sample = jnp.clip(jax.random.normal(key, array_shape, jnp.float32), -6.0, 6.0)
    return sample


def aligned_plan(key):
    plan_key = jax.random.fold_in(key, 7301)
    block_shape = (NBLK, 1, KVH)
    marked = jax.random.randint(jax.random.fold_in(plan_key, 1), block_shape, 0, 2) == 0
    offset = jax.random.randint(jax.random.fold_in(plan_key, 2), block_shape, 0, BLOCK // 2)
    which_query = jax.random.randint(jax.random.fold_in(plan_key, 3), block_shape, 0, 2)
    own_higher = jax.random.randint(jax.random.fold_in(plan_key, 4), block_shape, 0, 2) == 1
    sign_table = (jax.random.randint(jax.random.fold_in(plan_key, 5), (NBLK, 1, KVH, HD), 0, 2) * 2 - 1).astype(jnp.float32)
    places = jnp.arange(BLOCK, dtype=jnp.int32)[None, :, None]
    own_hit = marked & (places == 2 * offset + 1)
    prev_hit = marked & (places == 2 * offset)
    dim_index = jnp.arange(HD, dtype=jnp.int32)
    slow_dims = (dim_index % (HD // 2) >= HD // 4).astype(jnp.float32)
    pattern = sign_table * slow_dims
    top_score = jax.random.uniform(jax.random.fold_in(plan_key, 6), block_shape, jnp.float32, 68.0, 80.0)
    score_gap = jax.random.uniform(jax.random.fold_in(plan_key, 7), block_shape, jnp.float32, 3.0, 8.0)
    head_root = math.sqrt(HD)
    scale_query = jnp.sqrt(2.0 * top_score / head_root)
    own_score = jnp.where(own_higher, top_score, top_score - score_gap)
    prev_score = jnp.where(own_higher, top_score - score_gap, top_score)
    own_level = own_score / (scale_query * head_root / 2.0)
    prev_level = prev_score / (scale_query * head_root / 2.0)
    return (own_hit, prev_hit, which_query, pattern, slow_dims, scale_query, own_level, prev_level)


def draw_key_heads(key, part):
    own_hit, prev_hit, which_query, pattern, slow_dims, scale_query, own_level, prev_level = aligned_plan(key)
    filler = background(jax.random.fold_in(key, 31), (NBLK, BLOCK, KVH, HD))
    key_level = jnp.where(own_hit, own_level, prev_level)
    aligned = key_level[..., None] * pattern + filler * (1.0 - slow_dims)
    hit_any = own_hit | prev_hit
    values = jnp.where(hit_any[..., None], aligned, filler)
    return values.reshape(LENGTH, KVH * HD).astype(jnp.bfloat16)


def draw_queries(key, part):
    own_hit, prev_hit, which_query, pattern, slow_dims, scale_query, own_level, prev_level = aligned_plan(key)
    filler = background(jax.random.fold_in(key, 37), (NBLK, BLOCK, H, HD))
    head_parity = (jnp.arange(H, dtype=jnp.int32) % 2)[None, None, :]
    query_hit = jnp.repeat(own_hit, 2, axis=2) & (jnp.repeat(which_query, 2, axis=2) == head_parity)
    pattern_heads = jnp.repeat(pattern, 2, axis=2)
    scale_heads = jnp.repeat(scale_query, 2, axis=2)
    aligned = scale_heads[..., None] * pattern_heads
    values = jnp.where(query_hit[..., None], aligned, filler)
    return values.reshape(LENGTH, H * HD).astype(jnp.bfloat16)


def steps_of(key, extent, pieces, low, high):
    level = 1.0
    for axis_at, shards_of in pieces:
        draws = jax.random.uniform(jax.random.fold_in(jax.random.fold_in(key, 6), axis_at), (shards_of,), jnp.float32, low / len(pieces), high / len(pieces))
        level = level * jnp.repeat(jnp.exp(draws), extent[axis_at] // shards_of).reshape((-1,) + (1,) * (len(extent) - 1 - axis_at))
    return level


def length_profile(number_of, total, most, lean):
    portions = [(1 << 20) // math.isqrt(standing ** lean) + 1 for standing in range(2, number_of + 1)]
    spare, given = total - most - (number_of - 1), [1] * (number_of - 1)
    while spare > 0:
        free = [i for i in range(number_of - 1) if given[i] < most]
        pool, left = sum([portions[i] for i in free]), spare
        for i in free:
            more = min(most - given[i], max(1, left * portions[i] // pool), spare)
            given[i] = given[i] + more
            spare = spare - more
    return np.array([most] + given)


def ragged_sizes(own_key, number_of, total, most, lean):
    if number_of == 2:
        one = jax.random.randint(own_key, (), max(1, total - most), min(most, total - 1) + 1)
        return jnp.stack([one, total - one])
    tallies = jnp.asarray(length_profile(number_of, total, most, lean), jnp.int32)
    twos = (number_of - 1) // 2
    source_of, taker = tallies[1:1 + 2 * twos:2], tallies[2:2 + 2 * twos:2]
    room = jnp.minimum(source_of - 1, most - taker)
    moved = jax.random.randint(jax.random.fold_in(own_key, 1), (twos,), 0, 1 << 20) % (room + 1)
    tallies = tallies.at[1:1 + 2 * twos:2].set(source_of - moved).at[2:2 + 2 * twos:2].set(taker + moved)
    return tallies[jax.random.permutation(jax.random.fold_in(own_key, 2), number_of)]


def bell_draw(stream_key, dims, scale, reach, split=(), kind=jnp.bfloat16):
    array = jax.random.normal(stream_key, dims, jnp.float32) * scale
    if len(split) > 0:
        array = steps_of(stream_key, dims, split, -0.22, 0.18) * array
    return jnp.clip(array, min=-reach, max=reach).astype(kind)


def setup_inputs(seed: int = 0, part: int = 0) -> dict:
    seeds = jax.random.split(jax.random.key(seed), 11)
    part_keys = jax.random.split(jax.random.fold_in(seeds[10], part), 11)
    return {
        "residual": bell_draw(part_keys[0], (LENGTH, D), 1.0, 6.0, ((0, 16),)),
        "queries": draw_queries(jax.random.fold_in(jax.random.fold_in(seeds[10], part), 71), part),
        "key_heads": draw_key_heads(jax.random.fold_in(jax.random.fold_in(seeds[10], part), 71), part),
        "value_heads": bell_draw(part_keys[3], (LENGTH, KVH * HD), 1.0, 6.0, ((0, 4), (1, 4))),
        "doc_blocks": ragged_sizes(part_keys[4], DOCS, NBLK, MOST_BLK, 2).astype(jnp.int32),
        "out_weight": draw_out_weight(jax.random.fold_in(seeds[10], 71), part),
        "post_gain": jnp.clip(1.0 + 0.18 * jax.random.normal(seeds[6], (D,), jnp.float32), 0.1, 1.9),
        "ffn_gain": jnp.clip(1.0 + 0.18 * jax.random.normal(seeds[7], (D,), jnp.float32), 0.1, 1.9),
        "gate_weight": bell_draw(seeds[8], (D, FF), D ** -0.5, 0.09375, ((0, 4), (1, 4))),
        "up_weight": bell_draw(seeds[9], (D, FF), D ** -0.5, 0.09375, ((0, 4), (1, 4))),
    }


SOFT_CAP = 50.0
NORM_EPS = 1e-06
ROPE_BASE = 10000.0

def rope_angles(positions, head_size):
    halfway = head_size // 2
    frequency = ROPE_BASE ** (-(jnp.arange(halfway, dtype=jnp.float32) * 2.0) / head_size)
    angles = positions.astype(jnp.float32)[:, None] * frequency[None, :]
    return (jnp.cos(angles), jnp.sin(angles))

def rotate(heads_in, cosine, sine_value, head_size):
    rows_here = heads_in.shape[0]
    reshaped = heads_in.astype(jnp.float32).reshape(rows_here, -1, head_size)
    leading = reshaped[:, :, :head_size // 2]
    trailing = reshaped[:, :, head_size // 2:]
    cos_wide = cosine[:, None, :]
    sin_wide = sine_value[:, None, :]
    turned = jnp.concatenate([leading * cos_wide - trailing * sin_wide, trailing * cos_wide + leading * sin_wide], axis=2)
    return turned.reshape(rows_here, -1).astype(jnp.bfloat16)

def doc_of(positions, doc_blocks):
    doc_ends = jnp.cumsum(doc_blocks)
    passed = positions[:, None] // BLOCK >= doc_ends[None, :]
    return lax.optimization_barrier(jnp.sum(passed.astype(jnp.int32), axis=1)).astype(jnp.int32)

def rms_scale(values):
    return values * lax.rsqrt(lax.optimization_barrier(jnp.mean(values * values, axis=-1, keepdims=True)) + NORM_EPS)

def gelu_gate(gate_sum, up_sum):
    return (jax.nn.gelu(gate_sum, approximate=True) * up_sum).astype(jnp.bfloat16)

def attend(running, query_rows, query_pos, query_doc, key_rows, value_rows, key_pos, key_doc, score_scale):
    scores = lax.dot_general(query_rows, key_rows, (((1,), (1,)), ((), ())), preferred_element_type=jnp.float32) * score_scale
    capped = SOFT_CAP * jnp.tanh(scores / SOFT_CAP)
    visible = (key_pos[None, :] <= query_pos[:, None]) & (key_doc[None, :] == query_doc[:, None])
    weights = jnp.where(visible, jnp.exp(capped), 0.0).astype(jnp.bfloat16)
    numerator = running[0] + jnp.dot(weights, value_rows, preferred_element_type=jnp.float32)
    denominator = running[1] + lax.optimization_barrier(jnp.sum(weights.astype(jnp.float32), axis=1))
    return (numerator, denominator)

def reference(residual, queries, key_heads, value_heads, doc_blocks, out_weight, post_gain, ffn_gain, gate_weight, up_weight):
    length = residual.shape[0]
    positions = jnp.arange(length, dtype=jnp.int32)
    doc_ids = doc_of(positions, doc_blocks)
    cosine, sine_value = rope_angles(positions, HD)
    query_rot = rotate(queries, cosine, sine_value, HD).reshape(length, H, HD)
    key_rot = rotate(key_heads, cosine, sine_value, HD).reshape(length, KVH, HD)
    value_split = value_heads.reshape(length, KVH, HD)
    weight_split = out_weight.reshape(H, HD, D)
    score_scale = HD ** (-0.5)

    def one_head(summed, head_index):
        query_head = lax.dynamic_index_in_dim(query_rot, head_index, 1, keepdims=False)
        key_head = lax.dynamic_index_in_dim(key_rot, head_index // 2, 1, keepdims=False)
        value_head = lax.dynamic_index_in_dim(value_split, head_index // 2, 1, keepdims=False)

        def one_block(block_args):
            query_rows, query_pos, query_doc = block_args
            empty_sums = (jnp.zeros((TOK_CTX, HD), jnp.float32), jnp.zeros((TOK_CTX,), jnp.float32))
            numerator, denominator = attend(empty_sums, query_rows, query_pos, query_doc, key_head, value_head, positions, doc_ids, score_scale)
            return (numerator / denominator[:, None]).astype(jnp.bfloat16)
        attended = lax.map(one_block, (query_head.reshape(-1, TOK_CTX, HD), positions.reshape(-1, TOK_CTX), doc_ids.reshape(-1, TOK_CTX)))
        attended = attended.reshape(length, HD)
        head_weight = lax.dynamic_index_in_dim(weight_split, head_index, 0, keepdims=False)
        head_term = jnp.dot(attended, head_weight, preferred_element_type=jnp.float32).astype(jnp.bfloat16)
        head_term = lax.optimization_barrier(head_term)
        return (summed + head_term.astype(jnp.float32), None)
    attn_sum, _ = lax.scan(one_head, jnp.zeros((length, D), jnp.float32), jnp.arange(H, dtype=jnp.int32))
    mixed_stream = (residual.astype(jnp.float32) + rms_scale(attn_sum) * post_gain).astype(jnp.bfloat16)
    ffn_input = (rms_scale(mixed_stream.astype(jnp.float32)) * ffn_gain).astype(jnp.bfloat16)
    gate_sum = jnp.dot(ffn_input, gate_weight, preferred_element_type=jnp.float32)
    up_sum = jnp.dot(ffn_input, up_weight, preferred_element_type=jnp.float32)
    ffn_hidden = gelu_gate(gate_sum, up_sum)
    return (mixed_stream, ffn_hidden)
```

```python
import jax
import jax.numpy as jnp
from jax import lax
from jax.sharding import PartitionSpec as P

BLOCK = 32


SOFT_CAP = 50.0
NORM_EPS = 1e-06
ROPE_BASE = 10000.0


def partner_2(value, axis, apart):
    mask = 2**apart
    pairs = [(source, source ^ mask) for source in range(lax.axis_size(axis))]
    return lax.ppermute(value, axis, pairs)


def rope_angles(positions, head_size):
    halfway = head_size // 2
    frequency = ROPE_BASE ** (-(jnp.arange(halfway, dtype=jnp.float32) * 2.0) / head_size)
    angles = positions.astype(jnp.float32)[:, None] * frequency[None, :]
    return (jnp.cos(angles), jnp.sin(angles))


def rotate(heads_in, cosine, sine_value, head_size):
    rows_here = heads_in.shape[0]
    reshaped = heads_in.astype(jnp.float32).reshape(rows_here, -1, head_size)
    leading = reshaped[:, :, : head_size // 2]
    trailing = reshaped[:, :, head_size // 2 :]
    cos_wide = cosine[:, None, :]
    sin_wide = sine_value[:, None, :]
    turned = jnp.concatenate(
        [leading * cos_wide - trailing * sin_wide, trailing * cos_wide + leading * sin_wide], axis=2
    )
    return turned.reshape(rows_here, -1).astype(jnp.bfloat16)


def doc_of(positions, doc_blocks):
    doc_ends = jnp.cumsum(doc_blocks)
    passed = positions[:, None] // BLOCK >= doc_ends[None, :]
    return jnp.sum(passed.astype(jnp.int32), axis=1)


def rms_scale(values):
    return values * lax.rsqrt(jnp.mean(values * values, axis=-1, keepdims=True) + NORM_EPS)


def gelu_gate(gate_sum, up_sum):
    return (jax.nn.gelu(gate_sum, approximate=True) * up_sum).astype(jnp.bfloat16)


def attend(query_rows, query_pos, query_doc, key_rows, value_rows, key_pos, key_doc, score_scale):
    scores = (
        lax.dot_general(
            query_rows, key_rows, (((1,), (1,)), ((), ())), preferred_element_type=jnp.float32
        )
        * score_scale
    )
    capped = SOFT_CAP * jnp.tanh(scores / SOFT_CAP)
    visible = (key_pos[None, :] <= query_pos[:, None]) & (key_doc[None, :] == query_doc[:, None])
    weights = jnp.where(visible, jnp.exp(capped), 0.0).astype(jnp.bfloat16)
    numerator = jnp.dot(weights, value_rows, preferred_element_type=jnp.float32)
    denominator = jnp.sum(weights.astype(jnp.float32), axis=1)
    return (numerator, denominator)


def join_halves(own_part, other_part, own_first):
    return jnp.where(
        own_first,
        jnp.concatenate([own_part, other_part], axis=2),
        jnp.concatenate([other_part, own_part], axis=2),
    )


def relay_fits():
    return lax.axis_size("ctx") == 4 and lax.axis_size("dp") == 2


def relay_weights(gate_weight, up_weight):
    if not relay_fits():
        return None
    rows = gate_weight.shape[0]
    cut = -(-rows // 256) * 128
    first_part = lax.axis_index("dp") == 0
    carried = jnp.where(first_part, gate_weight, up_weight)
    far = [partner_2(carried[:cut], "ctx", 1), partner_2(carried[cut:], "ctx", 1)]
    near = [partner_2(weight, "ctx", 0) for weight in (gate_weight, up_weight)]
    return near, far


def hold_far(attended, relayed):
    if relayed is None:
        return attended, None
    near, far = relayed
    attended, near, far = lax.optimization_barrier((attended, near, far))
    swapped = [partner_2(piece, "dp", 0) for piece in far]
    far_near = [partner_2(piece, "ctx", 0) for piece in far]
    return attended, (near, far, swapped, far_near)


def hold_swapped(attn_rows, relayed):
    if relayed is None:
        return attn_rows, None
    near, far, swapped, far_near = relayed
    attn_rows, swapped, far_near = lax.optimization_barrier((attn_rows, swapped, far_near))
    swapped_near = [partner_2(piece, "ctx", 0) for piece in swapped]
    return attn_rows, (near, (far, swapped), (far_near, swapped_near))


def project(rows_in, gate_weight, up_weight, relayed):
    if relayed is None:
        return tuple(
            jnp.dot(
                rows_in,
                lax.all_gather(weight, "ctx", axis=0, tiled=True),
                preferred_element_type=jnp.float32,
            )
            for weight in (gate_weight, up_weight)
        )
    depth = gate_weight.shape[0]
    here = lax.axis_index("ctx")

    def term(owner, offset, weight):
        columns = lax.dynamic_slice_in_dim(rows_in, owner * depth + offset, weight.shape[0], axis=1)
        return jnp.dot(columns, weight, preferred_element_type=jnp.float32)

    near, across, across_near = relayed
    gate_sum = term(here, 0, gate_weight) + term(here ^ 1, 0, near[0])
    up_sum = term(here, 0, up_weight) + term(here ^ 1, 0, near[1])
    sums = []
    for which in range(2):
        total = 0.0
        for owner, pieces in ((here ^ 2, across[which]), (here ^ 3, across_near[which])):
            offset = 0
            for piece in pieces:
                total = total + term(owner, offset, piece)
                offset += piece.shape[0]
        sums.append(total)
    first_part = lax.axis_index("dp") == 0
    gate_sum = gate_sum + jnp.where(first_part, sums[0], sums[1])
    up_sum = up_sum + jnp.where(first_part, sums[1], sums[0])
    return gate_sum, up_sum


def per_device(
    residual,
    queries,
    key_heads,
    value_heads,
    doc_blocks,
    out_weight,
    post_gain,
    ffn_gain,
    gate_weight,
    up_weight,
):
    relayed = relay_weights(gate_weight, up_weight)
    tok_rows = queries.shape[0]
    head_size = queries.shape[1]
    score_scale = head_size ** (-0.5)
    query_pos = lax.axis_index("ctx") * tok_rows + jnp.arange(tok_rows, dtype=jnp.int32)
    query_doc = doc_of(query_pos, doc_blocks)
    cosine, sine_value = rope_angles(query_pos, head_size)
    query_rot = rotate(queries, cosine, sine_value, head_size)
    stacked = jnp.stack([key_heads, value_heads])
    own_first = lax.axis_index("tensor") % 2 == 0
    partner = partner_2(stacked, "tensor", 0)
    joined = join_halves(stacked, partner, own_first)
    key_rot = rotate(joined[0], cosine, sine_value, head_size)
    shard_pair = (
        lax.all_gather(key_rot, "ctx", axis=0, tiled=True),
        lax.all_gather(joined[1], "ctx", axis=0, tiled=True),
    )
    key_pos = jnp.arange(shard_pair[0].shape[0], dtype=jnp.int32)
    numerator, denominator = attend(
        query_rot,
        query_pos,
        query_doc,
        shard_pair[0],
        shard_pair[1],
        key_pos,
        doc_of(key_pos, doc_blocks),
        score_scale,
    )
    attended = (numerator / denominator[:, None]).astype(jnp.bfloat16)
    attended, relayed = hold_far(attended, relayed)
    attn_rows = lax.psum_scatter(
        jnp.dot(attended, out_weight, preferred_element_type=jnp.float32).astype(jnp.bfloat16),
        "tensor",
        scatter_dimension=0,
        tiled=True,
    ).astype(jnp.float32)
    attn_rows, relayed = hold_swapped(attn_rows, relayed)
    mixed_stream = (residual.astype(jnp.float32) + rms_scale(attn_rows) * post_gain).astype(
        jnp.bfloat16
    )
    ffn_input = (rms_scale(mixed_stream.astype(jnp.float32)) * ffn_gain).astype(jnp.bfloat16)
    gathered_rows = lax.all_gather(ffn_input, "tensor", axis=0, tiled=True)
    gate_part, up_part = project(gathered_rows, gate_weight, up_weight, relayed)
    ffn_hidden = gelu_gate(gate_part, up_part)
    return (mixed_stream, ffn_hidden)


def solution(mesh):
    in_specs = (
        P(("dp", "ctx", "tensor"), None),
        P(("dp", "ctx"), "tensor"),
        P(("dp", "ctx"), "tensor"),
        P(("dp", "ctx"), "tensor"),
        P("dp"),
        P("tensor", None),
        P(),
        P(),
        P("ctx", "tensor"),
        P("ctx", "tensor"),
    )
    out_specs = (P(("dp", "ctx", "tensor"), None), P(("dp", "ctx"), "tensor"))
    return jax.shard_map(
        per_device, mesh=mesh, in_specs=in_specs, out_specs=out_specs, check_vma=False
    )
```
